32 devices in a mesh: ri: 2 (over y), mu: 4 (over x, core), nu: 4 (over z).
Axes of the slice: x: 2, y: 2, z: 4, core: 2. Of those that a mesh axis runs over, the one named last changes fastest.
Arguments:
- three_center: bfloat16 [8, 2304, 128, 128], P('ri', ('mu', 'nu')), may hold values from -0.15625 to 0.15625
- block_pairs: int32 [2304, 2], P(('mu', 'nu')), may hold values from -1 to 95, as said below
- occ_factor: bfloat16 [12288, 128], P(('mu', 'nu')), may hold values from -6 to 6
- virt_density: bfloat16 [12288, 12288], P(('mu', 'nu'), 'ri'), may hold values from -0.0546875 to 0.0546875
- block_sizes: int32 [96], replicated, may hold values from 96 to 128
- occ_mask: int32 [96], replicated, may hold values 0 or 1
- virt_mask: int32 [96, 96], replicated, may hold values 0 or 1
Outputs:
- transformed: bfloat16 [8, 12288, 128], P('ri', ('mu', 'nu'))
The draws below stay inside these ranges and needn't reach their ends.
Inputs may be any that keep to these rules, and one draw needn't show every extreme that they name: `block_pairs`: slots k in [d * 144, (d + 1) * 144) belong to device d of mu+nu; a live slot holds a mu block of that device's mu range (the range of 24 blocks of its mu index) and any nu block; empty slots hold -1 in both columns, and the live slots of a device come first. Every mu block appears in exactly 12 live slots, with distinct nu blocks. A device holds at most 144 live slots, and in every mu range some device holds exactly 144.
All inputs are finite; a program needn't handle non-finite values.
Results may differ from the reference program's by a relative error of at most 0.015.
Values may be sent and summed in bfloat16 or wider, within the bound.
No kernel may reach another device: no remote copies, remote signals or barrier semaphores. Data moves between devices by JAX's collectives and lax.ppermute only.
A program may use at most 192 MiB of HBM per device.

```python
import jax
import jax.numpy as jnp
from jax import lax

BS = 128
NB = 96
KB = 12
OCC = 128
N = 12288
RI = 8
GRID_MU = 4
GRID_NU = 4
ROWPAIRS = 288
CAP = 144
PAIRS = 2304


def draw_block_pairs(key, part):
    keys = jax.random.split(key, 4)
    band = NB
    band_scores = jax.random.randint(keys[0], (NB, band), 0, 1 << 20) * band + jnp.arange(band, dtype=jnp.int32)[None, :]
    picked = jnp.argsort(band_scores, axis=1)[:, :KB].astype(jnp.int32)
    offsets = picked - band // 2
    nu_blocks = (jnp.arange(NB, dtype=jnp.int32)[:, None] + offsets) % NB
    mu_blocks = jnp.broadcast_to(jnp.arange(NB, dtype=jnp.int32)[:, None], (NB, KB))
    mu_rows = mu_blocks.reshape(GRID_MU, ROWPAIRS)
    nu_rows = nu_blocks.reshape(GRID_MU, ROWPAIRS)
    pair_scores = jax.random.randint(keys[1], (GRID_MU, ROWPAIRS), 0, 1 << 20) * ROWPAIRS + jnp.arange(ROWPAIRS, dtype=jnp.int32)[None, :]
    shuffle = jnp.argsort(pair_scores, axis=1).astype(jnp.int32)
    mu_rows = jnp.take_along_axis(mu_rows, shuffle, axis=1)
    nu_rows = jnp.take_along_axis(nu_rows, shuffle, axis=1)
    others = GRID_NU - 1
    rest = ROWPAIRS - CAP
    base = rest // others
    remain = rest % others
    other_index = jnp.arange(others, dtype=jnp.int32)
    counts_other = base + (other_index < remain).astype(jnp.int32)
    halves = others // 2
    shifts = jax.random.randint(keys[2], (GRID_MU, halves), 0, base // 2 + 1)
    delta = jnp.zeros((GRID_MU, others), jnp.int32)
    delta = delta.at[:, 0:2 * halves:2].add(shifts)
    delta = delta.at[:, 1:2 * halves:2].add(-shifts)
    counts_other = counts_other[None, :] + delta
    special = jax.random.randint(keys[3], (GRID_MU,), 0, GRID_NU)
    position = jnp.arange(GRID_NU, dtype=jnp.int32)[None, :]
    source = jnp.clip(position - (position > special[:, None]).astype(jnp.int32), 0, others - 1)
    counts = jnp.where(position == special[:, None], CAP, jnp.take_along_axis(counts_other, source, axis=1))
    starts = jnp.cumsum(counts, axis=1) - counts
    slot_index = jnp.arange(CAP, dtype=jnp.int32)
    slot_live = slot_index[None, None, :] < counts[:, :, None]
    where_index = jnp.clip(starts[:, :, None] + slot_index[None, None, :], 0, ROWPAIRS - 1).reshape(GRID_MU, GRID_NU * CAP)
    mu_pick = jnp.take_along_axis(mu_rows, where_index, axis=1).reshape(GRID_MU, GRID_NU, CAP)
    nu_pick = jnp.take_along_axis(nu_rows, where_index, axis=1).reshape(GRID_MU, GRID_NU, CAP)
    mu_out = jnp.where(slot_live, mu_pick, -1)
    nu_out = jnp.where(slot_live, nu_pick, -1)
    return jnp.stack([mu_out, nu_out], axis=-1).reshape(PAIRS, 2).astype(jnp.int32)


def set_ends(entries, stream_key, low, top_value):
    longest = entries.shape.index(max(entries.shape))
    spots = []
    for shift in (0, 1):
        where = [jax.random.randint(jax.random.fold_in(stream_key, axis), (), 0, length) for axis, length in enumerate(entries.shape)]
        where[longest] = (where[longest] + shift) % entries.shape[longest]
        spots.append(tuple(where))
    return entries.at[spots[0]].set(low).at[spots[1]].set(top_value)


def block_scale(rng, shape, pieces, smallest, high):
    factor_of = 1.0
    for dim, blocks in pieces:
        steps = jax.random.uniform(jax.random.fold_in(jax.random.fold_in(rng, 6), dim), (blocks,), jnp.float32, smallest / len(pieces), high / len(pieces))
        factor_of = factor_of * jnp.repeat(jnp.exp(steps), shape[dim] // blocks).reshape((-1,) + (1,) * (len(shape) - 1 - dim))
    return factor_of


def scatter_about(own_key, shape, width, most, cuts=(), kind=jnp.bfloat16):
    loudness = block_scale(own_key, shape, cuts, -0.22, 0.18) if cuts else 1.0
    values = jax.random.normal(own_key, shape, jnp.float32) * width * loudness
    return jnp.minimum(jnp.maximum(values, -most), most).astype(kind)


def setup_inputs(seed: int = 0) -> dict:
    streams_of = jax.random.split(jax.random.key(seed), 8)
    three_center = scatter_about(streams_of[0], (RI, PAIRS, BS, BS), (KB * BS) ** -0.5, 0.15625, ((0, 2), (1, 16)))
    block_pairs = draw_block_pairs(jax.random.fold_in(streams_of[7], 71), 0)
    occ_factor = scatter_about(streams_of[2], (N, OCC), 1.0, 6.0, ((0, 16),))
    virt_density = scatter_about(streams_of[3], (N, N), N ** -0.5, 0.0546875, ((0, 16), (1, 2)))
    block_sizes = set_ends(jax.random.randint(streams_of[4], (NB,), BS * 3 // 4, BS + 1), jax.random.fold_in(streams_of[4], 1), BS * 3 // 4, BS).astype(jnp.int32)
    occ_mask = set_ends((jax.random.randint(streams_of[5], (NB,), 0, 4) < 3).astype(jnp.int32), jax.random.fold_in(streams_of[5], 1), 0, 1)
    virt_mask = set_ends((jax.random.randint(streams_of[6], (NB, NB), 0, 4) < 3).astype(jnp.int32), jax.random.fold_in(streams_of[6], 1), 0, 1)
    return {"three_center": three_center, "block_pairs": block_pairs, "occ_factor": occ_factor, "virt_density": virt_density, "block_sizes": block_sizes, "occ_mask": occ_mask, "virt_mask": virt_mask}


def reference(three_center, block_pairs, occ_factor, virt_density, block_sizes, occ_mask, virt_mask):
    total_rows = NB * BS
    inside = jnp.arange(BS, dtype=jnp.int32)[None, :] < block_sizes[:, None]
    keep_occ = (inside & (occ_mask[:, None] > 0)).reshape(total_rows)
    occ_kept = jnp.where(keep_occ[:, None], occ_factor, jnp.zeros((), occ_factor.dtype))
    keep_virt = (virt_mask[:, None, :, None] > 0) & inside[:, :, None, None] & inside[None, None, :, :]
    virt_kept = jnp.where(keep_virt, virt_density.reshape(NB, BS, NB, BS), jnp.zeros((), virt_density.dtype))
    virt_kept = virt_kept.reshape(total_rows, total_rows)
    slot_live = (block_pairs[:, 0] >= 0).astype(jnp.float32)
    mu_block = jnp.clip(block_pairs[:, 0], 0, NB - 1).astype(jnp.int32)
    nu_block = jnp.clip(block_pairs[:, 1], 0, NB - 1).astype(jnp.int32)
    occ_blocks = occ_kept.reshape(NB, BS, OCC)[nu_block].astype(jnp.float32)

    def half_transform(ri_slab):
        products = jnp.einsum("kab,kbo->kao", ri_slab.astype(jnp.float32), occ_blocks)
        products = products * slot_live[:, None, None]
        summed = jax.ops.segment_sum(products, mu_block, num_segments=NB)
        return summed.reshape(total_rows, OCC).astype(jnp.bfloat16)

    half_rows = lax.map(half_transform, three_center)

    def full_transform(slab_rows):
        return jnp.dot(virt_kept, slab_rows, preferred_element_type=jnp.float32).astype(jnp.bfloat16)

    return lax.map(full_transform, half_rows)
```

```python
import functools

import jax
import jax.numpy as jnp
from jax import lax
from jax.experimental import pallas as pl
from jax.experimental.pallas import tpu as pltpu
from jax.sharding import PartitionSpec as P

AXES = ("ri", "mu", "nu")
BF16 = jnp.bfloat16
F32 = jnp.float32


def half_kernel(n_out, slots, mu_ref, nu_ref, tc_ref, occ_ref, *rest):
    outs, acc = rest[:n_out], rest[n_out]
    step = pl.program_id(0)

    @pl.when(step == 0)
    def _():
        acc[...] = jnp.zeros_like(acc)

    def one(i, carry):
        k = step * slots + i
        acc[mu_ref[k]] += jnp.dot(
            tc_ref[0, i], occ_ref[nu_ref[k]], preferred_element_type=F32
        )
        return carry

    lax.fori_loop(0, slots, one, 0, unroll=4)

    @pl.when(step == pl.num_programs(0) - 1)
    def _():
        start = 0
        for out in outs:
            rows = out.shape[0]
            out[...] = acc[start : start + rows].astype(BF16)
            start += rows


def half_transform(three_center, p, mu_local, nu_at, occ_blocks, blocks_mu, cuts):
    cap, bs = three_center.shape[1], three_center.shape[2]
    occ_cols = occ_blocks.shape[-1]
    slots = cap // 4 if cap % 16 == 0 else cap
    n_out = len(cuts)
    return pl.pallas_call(
        functools.partial(half_kernel, n_out, slots),
        out_shape=[jax.ShapeDtypeStruct((c, bs, occ_cols), BF16) for c in cuts],
        grid_spec=pltpu.PrefetchScalarGridSpec(
            num_scalar_prefetch=2,
            grid=(cap // slots,),
            in_specs=[
                pl.BlockSpec((1, slots, bs, bs), lambda j, *_: (p, j, 0, 0)),
                pl.BlockSpec(occ_blocks.shape, lambda j, *_: (0, 0, 0)),
            ],
            out_specs=[
                pl.BlockSpec((c, bs, occ_cols), lambda j, *_: (0, 0, 0)) for c in cuts
            ],
            scratch_shapes=[pltpu.VMEM((blocks_mu + 1, bs, occ_cols), F32)],
        ),
        name=f"half_{p}",
    )(mu_local, nu_at, three_center, occ_blocks)


def virt_kernel(n_x, v_ref, *rest):
    xs, out = rest[:n_x], rest[n_x]
    width = xs[0].shape[1]
    both = jnp.concatenate([x[...] for x in xs], axis=1)
    y = jnp.dot(v_ref[...], both, preferred_element_type=F32)
    for t in range(n_x):
        out[t] = y[:, t * width : (t + 1) * width].astype(out.dtype)


def virt_transform(virt, col_block, xs, dtype, name):
    rows = virt.shape[0]
    depth, width = xs[0].shape
    tile = rows // 3 if rows % 24 == 0 else rows
    return pl.pallas_call(
        functools.partial(virt_kernel, len(xs)),
        out_shape=jax.ShapeDtypeStruct((len(xs), rows, width), dtype),
        grid=(rows // tile,),
        in_specs=[pl.BlockSpec((tile, depth), lambda i: (i, col_block))]
        + [pl.BlockSpec((depth, width), lambda i: (0, 0)) for _ in xs],
        out_specs=pl.BlockSpec((len(xs), tile, width), lambda i: (0, i, 0)),
        name=name,
    )(virt, *xs)


def keep_virt(block_sizes, virt_mask, bs, row_start, rows_dev, col_start, cols_dev):
    nb = block_sizes.shape[0]
    inside = (jnp.arange(bs, dtype=jnp.int32)[None, :] < block_sizes[:, None]).reshape(nb * bs)
    row_ids = row_start + jnp.arange(rows_dev, dtype=jnp.int32)
    block_pick = (row_ids[:, None] // bs == jnp.arange(nb, dtype=jnp.int32)[None, :]).astype(F32)
    mask_cols = lax.dynamic_slice_in_dim(virt_mask, col_start // bs, cols_dev // bs, axis=1)
    mask_rows = jnp.dot(block_pick, mask_cols.astype(F32)) > 0.5
    row_inside = lax.dynamic_slice_in_dim(inside, row_start, rows_dev)
    col_inside = lax.dynamic_slice_in_dim(inside, col_start, cols_dev).reshape(cols_dev // bs, bs)
    return (
        mask_rows[:, :, None] & col_inside[None, :, :] & row_inside[:, None, None]
    ).reshape(rows_dev, cols_dev)


def gather_occ(occ, n_mu, n_nu, group):
    pieces = {(0, 0): occ}
    outer = n_mu // group
    for d in range(1, outer):
        ring = [
            (g * group + c, ((g + d) % outer) * group + c)
            for g in range(outer)
            for c in range(group)
        ]
        pieces[(d, 0)] = lax.ppermute(occ, "mu", ring)
    near = jnp.stack([pieces[(d, 0)] for d in range(outer)])
    far = [near]
    for d in range(1, n_nu):
        far.append(lax.ppermute(near, "nu", [(z, (z + d) % n_nu) for z in range(n_nu)]))
    column = jnp.stack(far)
    whole = [column]
    for d in range(1, group):
        ring = [
            (g * group + c, g * group + (c + d) % group)
            for g in range(outer)
            for c in range(group)
        ]
        whole.append(lax.ppermute(column, "mu", ring))
    return jnp.stack(whole)


def sum_over_nu(part, n_nu, is_mid):
    mid = n_nu // 2
    acc = part
    for i in range(mid - 1):
        step = [(i, i + 1), (n_nu - 1 - i, n_nu - 2 - i)]
        acc = acc + lax.ppermute(acc, "nu", step)
    acc = acc + lax.ppermute(acc, "nu", [(mid - 1, mid), (mid, mid - 1)])
    for i in range(mid - 1, 0, -1):
        step = [(i, i - 1), (n_nu - 1 - i, n_nu - i)]
        got = lax.ppermute(acc, "nu", step)
        z = lax.axis_index("nu")
        acc = jnp.where((z == i - 1) | (z == n_nu - i), got, acc)
    return acc


def body_paired(three_center, block_pairs, occ_kept, virt_density, block_sizes, virt_mask, sizes):
    n_ri, n_mu, n_nu = sizes
    nb, bs = block_sizes.shape[0], three_center.shape[2]
    occ_cols = occ_kept.shape[1]
    n_p = three_center.shape[0]
    rows_dev, cols_dev = virt_density.shape
    group = n_mu // n_ri
    blocks_mu = nb // n_mu
    r, mu, nu = (lax.axis_index(a) for a in AXES)
    g, c = mu // group, mu % group

    gathered = gather_occ(occ_kept, n_mu, n_nu, group)
    occ_blocks = gathered.reshape(nb, bs, occ_cols)
    per_piece = occ_kept.shape[0] // bs
    nu_block = jnp.clip(block_pairs[:, 1], 0, nb - 1)
    piece = nu_block // per_piece
    mu_of, nu_of = piece // n_nu, piece % n_nu
    d_core = (c - mu_of % group) % group
    d_nu = (nu - nu_of) % n_nu
    d_outer = (g - mu_of // group) % n_ri
    nu_at = ((d_core * n_nu + d_nu) * n_ri + d_outer) * per_piece + nu_block % per_piece
    live = block_pairs[:, 0] >= 0
    mu_local = jnp.where(live, block_pairs[:, 0] - mu * blocks_mu, blocks_mu)

    row_start = (mu * n_nu + nu) * rows_dev
    width = cols_dev // group
    virts = []
    for u in range(group):
        col = ((c + u) % group) * width
        keep = keep_virt(block_sizes, virt_mask, bs, row_start, rows_dev, r * cols_dev + col, width)
        mine = lax.dynamic_slice_in_dim(virt_density, col, width, axis=1)
        mine = jnp.where(keep, mine, jnp.zeros((), BF16))
        if u:
            ring = [
                (gg * group + cc, gg * group + (cc + u) % group)
                for gg in range(n_ri)
                for cc in range(group)
            ]
            mine = lax.ppermute(mine, "mu", ring)
        virts.append(mine)

    half_blocks = blocks_mu // 2
    cuts_of = [[blocks_mu]] * n_p
    if blocks_mu % 2 == 0 and n_p > 1:
        cuts_of = [[half_blocks, half_blocks]] + [[blocks_mu]] * (n_p - 2) + [[half_blocks, half_blocks]]

    def swap(t):
        out = []
        for rr in range(n_ri):
            for gg in range(n_ri):
                for cc in range(group):
                    for z in range(n_nu):
                        src = (rr * n_mu + gg * group + cc) * n_nu + z
                        to_g = (rr + t) % n_ri
                        dst = (gg * n_mu + to_g * group + cc) * n_nu + z
                        out.append((src, dst))
        return out

    is_mid = None
    totals = []
    for p in range(n_p):
        parts = half_transform(three_center, p, mu_local, nu_at, occ_blocks, blocks_mu, cuts_of[p])
        sums = None
        for j, part in enumerate(parts):
            rows = part.shape[0] * bs
            x = sum_over_nu(part.reshape(rows, occ_cols), n_nu, is_mid)
            xs = [lax.ppermute(x, AXES, swap(t)) for t in range(n_ri)]
            ys = [virt_transform(v, j, xs, F32, f"virt_{p}_{j}_{u}") for u, v in enumerate(virts)]
            sums = ys if sums is None else [a + b for a, b in zip(sums, ys)]
        totals.append(sums)

    results = []
    batches = [list(range(n_p - 1)), [n_p - 1]] if n_p > 1 else [[0]]
    for batch in batches:
        total = jnp.stack([totals[p][0] for p in batch], axis=1)
        for u in range(1, group):
            away = jnp.stack([totals[p][u] for p in batch], axis=1).astype(BF16)
            ring = [
                (gg * group + (cc + u) % group, gg * group + cc)
                for gg in range(n_ri)
                for cc in range(group)
            ]
            total = total + lax.ppermute(away, "mu", ring).astype(F32)
        own = lax.dynamic_index_in_dim(total, (g - r) % n_ri, 0, keepdims=False)
        for u in range(1, n_ri):
            away = lax.dynamic_index_in_dim(total, (g - r - u) % n_ri, 0, keepdims=False).astype(BF16)
            got = lax.ppermute(away, "ri", [(a, (a + u) % n_ri) for a in range(n_ri)])
            own = own + got.astype(F32)
        results.append(own.astype(BF16))
    return jnp.concatenate(results, axis=0)


def body_wide(three_center, block_pairs, occ_kept, virt_density, block_sizes, virt_mask, sizes):
    n_ri, n_mu, n_nu = sizes
    nb, bs = block_sizes.shape[0], three_center.shape[2]
    occ_cols = occ_kept.shape[1]
    n_p = three_center.shape[0]
    rows_dev, cols_dev = virt_density.shape
    blocks_mu = nb // n_mu
    r, mu, nu = (lax.axis_index(a) for a in AXES)
    occ_blocks = lax.all_gather(occ_kept, ("mu", "nu"), axis=0, tiled=True).reshape(nb, bs, occ_cols)
    nu_at = jnp.clip(block_pairs[:, 1], 0, nb - 1)
    mu_local = jnp.where(block_pairs[:, 0] >= 0, block_pairs[:, 0] - mu * blocks_mu, blocks_mu)
    parts = [
        half_transform(three_center, p, mu_local, nu_at, occ_blocks, blocks_mu, [blocks_mu])[0]
        for p in range(n_p)
    ]
    half = jnp.stack(parts).reshape(n_p, blocks_mu * bs, occ_cols)
    half = lax.all_gather(lax.psum(half, "nu"), "mu", axis=1, tiled=True)
    half = lax.all_to_all(half, "ri", split_axis=1, concat_axis=0, tiled=True)
    row_start = (mu * n_nu + nu) * rows_dev
    keep = keep_virt(block_sizes, virt_mask, bs, row_start, rows_dev, r * cols_dev, cols_dev)
    virt = jnp.where(keep, virt_density, jnp.zeros((), BF16))
    out = jnp.einsum("sm,pmo->pso", virt, half, preferred_element_type=F32)
    return lax.psum_scatter(out.astype(BF16), "ri", scatter_dimension=0, tiled=True)


def body(three_center, block_pairs, occ_factor, virt_density, block_sizes, occ_mask, virt_mask):
    sizes = n_ri, n_mu, n_nu = tuple(lax.axis_size(a) for a in AXES)
    nb, bs = block_sizes.shape[0], three_center.shape[2]
    inside = jnp.arange(bs, dtype=jnp.int32)[None, :] < block_sizes[:, None]
    keep_occ = (inside & (occ_mask[:, None] > 0)).reshape(nb * bs)
    rows_occ = occ_factor.shape[0]
    start = (lax.axis_index("mu") * n_nu + lax.axis_index("nu")) * rows_occ
    keep_mine = lax.dynamic_slice_in_dim(keep_occ, start, rows_occ)
    occ_kept = jnp.where(keep_mine[:, None], occ_factor, jnp.zeros((), BF16))
    paired = n_mu % n_ri == 0 and n_nu % 2 == 0
    run = body_paired if paired else body_wide
    return run(three_center, block_pairs, occ_kept, virt_density, block_sizes, virt_mask, sizes)


def solution(mesh):
    in_specs = (
        P("ri", ("mu", "nu"), None, None),
        P(("mu", "nu"), None),
        P(("mu", "nu"), None),
        P(("mu", "nu"), "ri"),
        P(),
        P(),
        P(),
    )
    out_specs = P("ri", ("mu", "nu"), None)
    return jax.shard_map(body, mesh=mesh, in_specs=in_specs, out_specs=out_specs, check_vma=False)
```
